32 devices in a mesh: dp: 4 (over x, core), row: 4 (over z), col: 2 (over y).
Axes of the slice: x: 2, y: 2, z: 4, core: 2. Of those that a mesh axis runs over, the one named last changes fastest.
Arguments:
- hidden_in: float32 [1024, 32768], P('col', ('dp', 'row')), may hold values from -6 to 6
- lengths: int32 [64], P(('dp', 'row')), may hold values from 1 to 512, as said below
- ln1_gain: float32 [1024], P('col'), may hold values from 0.25 to 1.75
- ln1_shift: float32 [1024], P('col'), may hold values from -3 to 3
- w_qkv: bfloat16 [1024, 3072], P('row', 'col'), may hold values from -0.1875 to 0.1875
- bias_q: float32 [1024], P('col'), may hold values from -3 to 3
- bias_v: float32 [1024], P('col'), may hold values from -3 to 3
- w_out: bfloat16 [1024, 1024], P('col', 'row'), may hold values from -0.375 to 0.375
- bias_out: float32 [1024], P('col'), may hold values from -3 to 3
- ln2_gain: float32 [1024], P('col'), may hold values from 0.25 to 1.75
- ln2_shift: float32 [1024], P('col'), may hold values from -3 to 3
- w_up: bfloat16 [1024, 4096], P('row', 'col'), may hold values from -0.1875 to 0.1875
- bias_up: float32 [4096], P('col'), may hold values from -3 to 3
- w_down: bfloat16 [4096, 1024], P('col', 'row'), may hold values from -0.125 to 0.125
- bias_down: float32 [1024], P('col'), may hold values from -3 to 3
- cotangent: float32 [1024, 32768], P('col', ('dp', 'row')), may hold values from -6 to 6
Outputs:
- hidden_out: float32 [1024, 32768], P('col', ('dp', 'row'))
- grad_in: float32 [1024, 32768], P('col', ('dp', 'row'))
- grad_ln1_gain: float32 [1024], P('col')
- grad_ln1_shift: float32 [1024], P('col')
- grad_w_qkv: float32 [1024, 3072], P('row', 'col')
- grad_bias_q: float32 [1024], P('col')
- grad_bias_v: float32 [1024], P('col')
- grad_w_out: float32 [1024, 1024], P('col', 'row')
- grad_bias_out: float32 [1024], P('col')
- grad_ln2_gain: float32 [1024], P('col')
- grad_ln2_shift: float32 [1024], P('col')
- grad_w_up: float32 [1024, 4096], P('row', 'col')
- grad_bias_up: float32 [4096], P('col')
- grad_w_down: float32 [4096, 1024], P('col', 'row')
- grad_bias_down: float32 [1024], P('col')
The draws below stay inside these ranges and needn't reach their ends.
Inputs may be any that keep to these rules, and one draw needn't show every extreme that they name: `lengths`: each slot holds one sequence of this many tokens followed by padding; some slot of every index pair of dp and row is full.
All inputs are finite; a program needn't handle non-finite values.
Results may differ from the reference program's by a relative error of at most 0.019.
Values may be sent and summed in bfloat16 or wider, within the bound.
A program may use at most 192 MiB of HBM per device.

```python
import math
import jax
import jax.numpy as jnp
from jax import lax

D = 1024
HEADS = 16
HEAD = 64
FF = 4096
SLOT = 512
SEQ_DEV = 4
DP_SEQS = 16
SEQS = 64
TOKENS = 32768


def draw_lengths(key, part):
    index = jnp.arange(SEQS)
    band = index // DP_SEQS
    bands = SEQS // DP_SEQS
    reach = SLOT * (band + 1) // bands
    reach = jnp.maximum(reach, 1)
    drop = jax.random.randint(key, (SEQS,), 0, 1 << 20) % reach
    length = SLOT - drop
    length = jnp.where(index % SEQ_DEV == 0, SLOT, length)
    return length.astype(jnp.int32)


def steps_of(key, dims, split, low, top_value):
    def one(dim, parts):
        heights = jax.random.uniform(jax.random.fold_in(jax.random.fold_in(key, 6), dim), (parts,), jnp.float32, low / len(split), top_value / len(split))
        return jnp.repeat(jnp.exp(heights), dims[dim] // parts).reshape((-1,) + (1,) * (len(dims) - dim - 1))

    loudness = one(*split[0])
    for cut in split[1:]:
        loudness = loudness * one(*cut)
    return loudness


def scatter_about(own_key, shape, width, limit, cuts=(), kind=jnp.bfloat16):
    values = jax.random.normal(own_key, shape, jnp.float32) * width
    if len(cuts) > 0:
        values = steps_of(own_key, shape, cuts, -0.22, 0.18) * values
    return jnp.clip(values, min=-limit, max=limit).astype(kind)


def setup_inputs(seed: int = 0) -> dict:
    splits = jax.random.split(jax.random.key(seed), 17)
    hidden_in = scatter_about(splits[0], (D, TOKENS), 1.0, 6.0, ((0, 2), (1, 16)), jnp.float32)
    lengths = draw_lengths(jax.random.fold_in(splits[16], 71), 0)
    ln1_gain = jnp.clip(1.0 + 0.15 * jax.random.normal(splits[2], (D,), jnp.float32), 0.25, 1.75)
    ln1_shift = scatter_about(splits[3], (D,), 0.3, 3.0, ((0, 2),), jnp.float32)
    w_qkv = scatter_about(splits[4], (D, 3 * D), D ** -0.5, 0.1875, ((0, 4), (1, 2)))
    bias_q = scatter_about(splits[5], (D,), 0.5, 3.0, ((0, 2),), jnp.float32)
    bias_v = scatter_about(splits[6], (D,), 0.5, 3.0, ((0, 2),), jnp.float32)
    w_out = scatter_about(splits[7], (D, D), (D // 4) ** -0.5, 0.375, ((0, 2), (1, 4)))
    bias_out = scatter_about(splits[8], (D,), 0.5, 3.0, ((0, 2),), jnp.float32)
    ln2_gain = jnp.clip(1.0 + 0.15 * jax.random.normal(splits[9], (D,), jnp.float32), 0.25, 1.75)
    ln2_shift = scatter_about(splits[10], (D,), 0.3, 3.0, ((0, 2),), jnp.float32)
    w_up = scatter_about(splits[11], (D, FF), D ** -0.5, 0.1875, ((0, 4), (1, 2)))
    bias_up = scatter_about(splits[12], (FF,), 0.5, 3.0, ((0, 2),), jnp.float32)
    w_down = scatter_about(splits[13], (FF, D), (FF // 2) ** -0.5, 0.125, ((0, 2), (1, 4)))
    bias_down = scatter_about(splits[14], (D,), 0.5, 3.0, ((0, 2),), jnp.float32)
    cotangent = scatter_about(splits[15], (D, TOKENS), 1.0, 6.0, ((0, 2), (1, 16)), jnp.float32)
    return {"hidden_in": hidden_in, "lengths": lengths, "ln1_gain": ln1_gain, "ln1_shift": ln1_shift, "w_qkv": w_qkv, "bias_q": bias_q, "bias_v": bias_v, "w_out": w_out, "bias_out": bias_out, "ln2_gain": ln2_gain, "ln2_shift": ln2_shift, "w_up": w_up, "bias_up": bias_up, "w_down": w_down, "bias_down": bias_down, "cotangent": cotangent}


EPS = 1e-05
NEG = -1e+30
HIGH = lax.Precision.HIGHEST

@jax.custom_vjp
def low(v):
    return lax.optimization_barrier(v.astype(jnp.bfloat16)).astype(jnp.float32)

@jax.custom_vjp
def low_back(v):
    return v

def low_keep(v):
    return (low(v), None)

def low_pass(kept, grad):
    return (grad,)

def back_keep(v):
    return (v, None)

def back_low(kept, grad):
    return (low(grad),)
low.defvjp(low_keep, low_pass)
low_back.defvjp(back_keep, back_low)

def matmul(left, right):
    return jnp.dot(left, right, precision=HIGH, preferred_element_type=jnp.float32)

def layer_norm(value, gain, shift):
    mean = lax.optimization_barrier(jnp.mean(value, axis=-1, keepdims=True))
    var = lax.optimization_barrier(jnp.mean(value * value, axis=-1, keepdims=True)) - mean * mean
    return (value - mean) * lax.rsqrt(var + EPS) * gain + shift

def group_forward(block_in, lens, params):
    gain1, shift1, wqkv, bq, bv, wout, bout, gain2, shift2, wup, bup, wdown, bdown = params
    count = lens.shape[0]
    rows = block_in.shape[0]
    norm1 = low(layer_norm(block_in, gain1, shift1))
    mixed = low_back(matmul(norm1, wqkv)).reshape(rows, HEADS, 3, HEAD)
    query = low(mixed[:, :, 0] + bq.reshape(HEADS, HEAD)).reshape(count, SLOT, HEADS, HEAD)
    keys = low(mixed[:, :, 1]).reshape(count, SLOT, HEADS, HEAD)
    values = low(mixed[:, :, 2] + bv.reshape(HEADS, HEAD)).reshape(count, SLOT, HEADS, HEAD)
    slopes = jnp.exp2(-8.0 * (jnp.arange(HEADS).astype(jnp.float32) + 1.0) / HEADS)
    pos = jnp.arange(SLOT)
    offset = (pos[None, :] - pos[:, None]).astype(jnp.float32)
    raw = jnp.einsum('gqhd,gkhd->ghqk', query, keys, precision=HIGH) * 0.125
    raw = raw + slopes[None, :, None, None] * offset[None, None]
    scores = low_back(raw)
    visible = (pos[None, :] <= pos[:, None])[None] & (pos[None, None, :] < lens[:, None, None])
    scores = jnp.where(visible[:, None], scores, NEG)
    top = lax.optimization_barrier(jnp.max(scores, axis=-1, keepdims=True))
    expo = jnp.exp(scores - top)
    probs = expo / lax.optimization_barrier(jnp.sum(expo, axis=-1, keepdims=True))
    attn = jnp.einsum('ghqk,gkhd->gqhd', low(probs), values, precision=HIGH)
    attn = low(low_back(attn)).reshape(rows, D)
    hidden1 = block_in + low_back(matmul(attn, wout)) + bout
    norm2 = low(layer_norm(hidden1, gain2, shift2))
    act = low(jax.nn.gelu(low_back(matmul(norm2, wup)) + bup, approximate=True))
    return hidden1 + low_back(matmul(act, wdown)) + bdown

def reference(hidden_in, lengths, ln1_gain, ln1_shift, w_qkv, bias_q, bias_v, w_out, bias_out, ln2_gain, ln2_shift, w_up, bias_up, w_down, bias_down, cotangent):
    params = tuple((p.astype(jnp.float32) for p in (ln1_gain, ln1_shift, w_qkv, bias_q, bias_v, w_out, bias_out, ln2_gain, ln2_shift, w_up, bias_up, w_down, bias_down)))
    per = math.gcd(SEQS, max(1, 4096 // SLOT))
    steps = SEQS // per
    lens = lengths.reshape(steps, per)
    block_fn = jax.checkpoint(group_forward)

    def forward(value, weights):
        pieces = value.reshape(steps, per * SLOT, D)

        def step(carry, item):
            return (carry, block_fn(item[0], item[1], weights))
        _, outs = lax.scan(step, jnp.zeros((), jnp.float32), (pieces, lens))
        return outs.reshape(TOKENS, D)
    tokens_in = jnp.transpose(hidden_in.astype(jnp.float32))
    result, pull = jax.vjp(forward, tokens_in, params)
    grad_x, grads = pull(jnp.transpose(cotangent.astype(jnp.float32)))
    return (jnp.transpose(result), jnp.transpose(grad_x), grads[0], grads[1], grads[2], grads[3], grads[4], grads[5], grads[6], grads[7], grads[8], grads[9], grads[10], grads[11], grads[12])
```

```python
from functools import partial

import jax
import jax.numpy as jnp
from jax import lax
from jax.experimental import pallas as pl
from jax.experimental.pallas import tpu as pltpu
from jax.sharding import PartitionSpec as P

HEADS = 16
HEAD = 64


EPS = 1e-05
NEG = -1e30


def norm_forward(value, gain, shift):
    width = value.shape[1] * lax.axis_size("col")
    sums = lax.psum((jnp.sum(value, axis=1), jnp.sum(value * value, axis=1)), "col")
    mean = (sums[0] / width)[:, None]
    var = (sums[1] / width)[:, None] - mean * mean
    inverse = lax.rsqrt(var + EPS)
    normed = (value - mean) * inverse
    return (normed, inverse, (normed * gain + shift).astype(jnp.bfloat16))


def norm_backward(incoming, normed, inverse, gain):
    width = incoming.shape[1] * lax.axis_size("col")
    scaled = incoming * gain
    sums = lax.psum((jnp.sum(scaled, axis=1), jnp.sum(scaled * normed, axis=1)), "col")
    return inverse * (scaled - sums[0][:, None] / width - normed * sums[1][:, None] / width)


def gather_rows(value):
    return lax.all_gather(value, "col", axis=1, tiled=True)


def back_columns(value):
    return lax.psum_scatter(
        value.astype(jnp.bfloat16), "col", scatter_dimension=1, tiled=True
    ).astype(jnp.float32)


def slot_scores(slopes, query, keys, length):
    span = query.shape[0]
    pos = jnp.arange(span)
    offset = (pos[None, :] - pos[:, None]).astype(jnp.float32)
    raw = jnp.einsum("qhd,khd->hqk", query, keys, preferred_element_type=jnp.float32) * 0.125
    raw = raw + slopes[:, None, None] * offset[None]
    visible = (pos[None, :] <= pos[:, None]) & (pos[None, :] < length)
    return jnp.where(visible[None], raw, NEG)


def forward_slot(slopes, item):
    query, keys, values, length = item
    scores = slot_scores(slopes, query, keys, length)
    top = jnp.max(scores, axis=-1, keepdims=True)
    expo = jnp.exp(scores - top)
    total = jnp.sum(expo, axis=-1, keepdims=True)
    probs = expo / total
    attended = jnp.einsum(
        "hqk,khd->qhd", probs.astype(jnp.bfloat16), values, preferred_element_type=jnp.float32
    )
    return (attended, (top + jnp.log(total))[..., 0])


def backward_slot(slopes, item):
    query, keys, values, grad_out, lse, length = item
    scores = slot_scores(slopes, query, keys, length)
    probs = jnp.exp(scores - lse[..., None])
    grad_probs = jnp.einsum("qhd,khd->hqk", grad_out, values, preferred_element_type=jnp.float32)
    grad_values = jnp.einsum(
        "hqk,qhd->khd", probs.astype(jnp.bfloat16), grad_out, preferred_element_type=jnp.float32
    )
    inner = jnp.sum(probs * grad_probs, axis=-1, keepdims=True)
    grad_scores = (probs * (grad_probs - inner)).astype(jnp.bfloat16)
    grad_query = (
        jnp.einsum("hqk,khd->qhd", grad_scores, keys, preferred_element_type=jnp.float32) * 0.125
    )
    grad_keys = (
        jnp.einsum("hqk,qhd->khd", grad_scores, query, preferred_element_type=jnp.float32) * 0.125
    )
    return (grad_query, grad_keys, grad_values)


def wide_body(
    hidden_in,
    lengths,
    ln1_gain,
    ln1_shift,
    w_qkv,
    bias_q,
    bias_v,
    w_out,
    bias_out,
    ln2_gain,
    ln2_shift,
    w_up,
    bias_up,
    w_down,
    bias_down,
    cotangent,
):
    tokens_in = jnp.transpose(hidden_in)
    grad_given = jnp.transpose(cotangent)
    rows = tokens_in.shape[0]
    slots = lengths.shape[0]
    span = rows // slots
    heads_here = w_qkv.shape[1] // (3 * HEAD)
    head_ids = lax.axis_index("col") * heads_here + jnp.arange(heads_here)
    slopes = jnp.exp2(-8.0 * (head_ids.astype(jnp.float32) + 1.0) / HEADS)
    qkv_full, up_full, out_full, down_full = (
        lax.all_gather(w_qkv, "row", axis=0, tiled=True),
        lax.all_gather(w_up, "row", axis=0, tiled=True),
        lax.all_gather(w_out, "row", axis=1, tiled=True),
        lax.all_gather(w_down, "row", axis=1, tiled=True),
    )
    normed1, inverse1, low1 = norm_forward(tokens_in, ln1_gain, ln1_shift)
    rows1 = gather_rows(low1)
    mixed = jnp.dot(rows1, qkv_full, preferred_element_type=jnp.float32).reshape(
        rows, heads_here, 3, HEAD
    )
    query = (
        (mixed[:, :, 0] + bias_q.reshape(heads_here, HEAD))
        .astype(jnp.bfloat16)
        .reshape(slots, span, heads_here, HEAD)
    )
    keys = mixed[:, :, 1].astype(jnp.bfloat16).reshape(slots, span, heads_here, HEAD)
    values = (
        (mixed[:, :, 2] + bias_v.reshape(heads_here, HEAD))
        .astype(jnp.bfloat16)
        .reshape(slots, span, heads_here, HEAD)
    )
    attended, lse = lax.map(partial(forward_slot, slopes), (query, keys, values, lengths))
    attn_low = attended.reshape(rows, heads_here * HEAD).astype(jnp.bfloat16)
    projected = lax.psum_scatter(
        jnp.dot(attn_low, out_full, preferred_element_type=jnp.float32),
        "col",
        scatter_dimension=1,
        tiled=True,
    )
    hidden1 = tokens_in + projected + bias_out
    normed2, inverse2, low2 = norm_forward(hidden1, ln2_gain, ln2_shift)
    rows2 = gather_rows(low2)
    pre = jnp.dot(rows2, up_full, preferred_element_type=jnp.float32) + bias_up
    act, act_pull = jax.vjp(partial(jax.nn.gelu, approximate=True), pre)
    act_low = act.astype(jnp.bfloat16)
    down_terms = jnp.dot(act_low, down_full, preferred_element_type=jnp.float32)
    result = (
        hidden1
        + lax.psum_scatter(
            down_terms.astype(jnp.bfloat16), "col", scatter_dimension=1, tiled=True
        ).astype(jnp.float32)
        + bias_down
    )
    grad_low = grad_given.astype(jnp.bfloat16)
    grad_full = lax.all_gather(grad_low, "col", axis=1, tiled=True)
    grad_down = jnp.einsum("tf,td->fd", act_low, grad_full, preferred_element_type=jnp.float32)
    grad_act = jnp.einsum("td,fd->tf", grad_full, down_full, preferred_element_type=jnp.float32)
    grad_pre = act_pull(grad_act)[0]
    grad_pre_low = grad_pre.astype(jnp.bfloat16)
    grad_up = jnp.einsum("td,tf->df", rows2, grad_pre_low, preferred_element_type=jnp.float32)
    grad_norm2 = back_columns(
        jnp.einsum("tf,df->td", grad_pre_low, up_full, preferred_element_type=jnp.float32)
    )
    grad_hidden1 = grad_given + norm_backward(grad_norm2, normed2, inverse2, ln2_gain)
    branch_low = grad_hidden1.astype(jnp.bfloat16)
    grad_branch = lax.all_gather(branch_low, "col", axis=1, tiled=True)
    grad_outw = jnp.einsum("tc,td->cd", attn_low, grad_branch, preferred_element_type=jnp.float32)
    grad_attn = jnp.einsum(
        "td,cd->tc", grad_branch, out_full, preferred_element_type=jnp.float32
    ).astype(jnp.bfloat16)
    grad_attn = grad_attn.reshape(slots, span, heads_here, HEAD)
    grad_query, grad_keys, grad_values = lax.map(
        partial(backward_slot, slopes), (query, keys, values, grad_attn, lse, lengths)
    )
    stacked = jnp.stack((grad_query, grad_keys, grad_values), axis=3).reshape(
        rows, 3 * heads_here * HEAD
    )
    stacked_low = stacked.astype(jnp.bfloat16)
    grad_qkv = jnp.einsum("td,tc->dc", rows1, stacked_low, preferred_element_type=jnp.float32)
    grad_norm1 = back_columns(
        jnp.einsum("tc,dc->td", stacked_low, qkv_full, preferred_element_type=jnp.float32)
    )
    grad_input = grad_hidden1 + norm_backward(grad_norm1, normed1, inverse1, ln1_gain)
    small = lax.psum(
        (
            jnp.sum(grad_norm1 * normed1, axis=0),
            jnp.sum(grad_norm1, axis=0),
            jnp.sum(grad_query.reshape(rows, heads_here * HEAD), axis=0),
            jnp.sum(grad_values.reshape(rows, heads_here * HEAD), axis=0),
            jnp.sum(grad_hidden1, axis=0),
            jnp.sum(grad_norm2 * normed2, axis=0),
            jnp.sum(grad_norm2, axis=0),
            jnp.sum(grad_pre, axis=0),
            jnp.sum(grad_given, axis=0),
        ),
        ("dp", "row"),
    )
    local = (grad_qkv, grad_up, grad_outw, grad_down)
    whole = (
        lax.psum(local[0].astype(jnp.bfloat16), "dp").astype(jnp.float32),
        lax.psum(local[1].astype(jnp.bfloat16), "dp").astype(jnp.float32),
        lax.psum(local[2].astype(jnp.bfloat16), "dp").astype(jnp.float32),
        lax.psum(local[3].astype(jnp.bfloat16), "dp").astype(jnp.float32),
    )
    summed = (
        lax.psum_scatter(
            whole[0].astype(jnp.bfloat16), "row", scatter_dimension=0, tiled=True
        ).astype(jnp.float32),
        lax.psum_scatter(
            whole[1].astype(jnp.bfloat16), "row", scatter_dimension=0, tiled=True
        ).astype(jnp.float32),
        lax.psum_scatter(
            whole[2].astype(jnp.bfloat16), "row", scatter_dimension=1, tiled=True
        ).astype(jnp.float32),
        lax.psum_scatter(
            whole[3].astype(jnp.bfloat16), "row", scatter_dimension=1, tiled=True
        ).astype(jnp.float32),
    )
    return (
        jnp.transpose(result),
        jnp.transpose(grad_input),
        small[0],
        small[1],
        summed[0],
        small[2],
        small[3],
        summed[2],
        small[4],
        small[5],
        small[6],
        summed[1],
        small[7],
        summed[3],
        small[8],
    )


def slot_terms(slope, query, keys, length, first, block):
    span = first + block
    raw = lax.dot_general(
        keys[:, :span], query, (((0,), (0,)), ((), ())), preferred_element_type=jnp.float32
    )
    key_pos = lax.broadcasted_iota(jnp.int32, (span, 1), 0)
    bias = jnp.where(key_pos < length, slope * key_pos.astype(jnp.float32), NEG)
    key_all = lax.broadcasted_iota(jnp.int32, (span, block), 0)
    query_all = lax.broadcasted_iota(jnp.int32, (span, block), 1) + first
    return jnp.where(key_all <= query_all, raw + bias, NEG)


def attend_kernel(lengths, slopes, mixed_ref, attn_ref, lse_ref):
    length = lengths[pl.program_id(1)]
    span = mixed_ref.shape[2]
    block = span // 2
    for head in range(mixed_ref.shape[0]):
        slope = slopes[pl.program_id(0) * mixed_ref.shape[0] + head]
        for first in (0, block):
            end = first + block
            query = mixed_ref[head, :HEAD, first:end] * 0.125
            scores = slot_terms(slope, query, mixed_ref[head, HEAD : 2 * HEAD], length, first, block)
            top = jnp.max(scores, axis=0, keepdims=True)
            expo = jnp.exp(scores - top)
            total = jnp.sum(expo, axis=0, keepdims=True)
            attended = jnp.dot(
                mixed_ref[head, 2 * HEAD :, :end],
                expo.astype(jnp.bfloat16),
                preferred_element_type=jnp.float32,
            )
            attn_ref[head, :, first:end] = (attended / total).astype(jnp.bfloat16)
            lse_ref[head, :, first:end] = top + jnp.log(total)


def attend_back_kernel(lengths, slopes, mixed_ref, grad_ref, lse_ref, out_ref):
    length = lengths[pl.program_id(1)]
    span = mixed_ref.shape[2]
    block = span // 2
    over_queries = (((1,), (1,)), ((), ()))
    for head in range(mixed_ref.shape[0]):
        slope = slopes[pl.program_id(0) * mixed_ref.shape[0] + head]
        terms = []
        for first in (0, block):
            end = first + block
            query = mixed_ref[head, :HEAD, first:end] * 0.125
            grad = grad_ref[head, :, first:end]
            keys = mixed_ref[head, HEAD : 2 * HEAD]
            scores = slot_terms(slope, query, keys, length, first, block)
            probs = jnp.exp(scores - lse_ref[head, :, first:end])
            grad_probs = lax.dot_general(
                mixed_ref[head, 2 * HEAD :, :end],
                grad,
                (((0,), (0,)), ((), ())),
                preferred_element_type=jnp.float32,
            )
            inner = jnp.sum(probs * grad_probs, axis=0, keepdims=True)
            grad_scores = (probs * (grad_probs - inner)).astype(jnp.bfloat16)
            grad_query = jnp.dot(keys[:, :end], grad_scores, preferred_element_type=jnp.float32)
            out_ref[head, :HEAD, first:end] = (grad_query * 0.125).astype(jnp.bfloat16)
            terms.append(
                (
                    lax.dot_general(
                        query, grad_scores, over_queries, preferred_element_type=jnp.float32
                    ),
                    lax.dot_general(
                        grad,
                        probs.astype(jnp.bfloat16),
                        over_queries,
                        preferred_element_type=jnp.float32,
                    ),
                )
            )
        for which in (0, 1):
            low = HEAD * (1 + which)
            early, late = terms[0][which], terms[1][which]
            out_ref[head, low : low + HEAD, :block] = (early + late[:, :block]).astype(jnp.bfloat16)
            out_ref[head, low : low + HEAD, block:] = late[:, block:].astype(jnp.bfloat16)


HEADS_STEP = 2


def per_head(rows, span):
    return pl.BlockSpec((HEADS_STEP, rows, span), lambda h, s, *_: (h, 0, s))


def attend(lengths, slopes, mixed):
    heads, depth, rows = mixed.shape
    slots = lengths.shape[0]
    span = rows // slots
    return pl.pallas_call(
        attend_kernel,
        grid_spec=pltpu.PrefetchScalarGridSpec(
            num_scalar_prefetch=2,
            grid=(heads // HEADS_STEP, slots),
            in_specs=[per_head(depth, span)],
            out_specs=[per_head(HEAD, span), per_head(1, span)],
        ),
        out_shape=[
            jax.ShapeDtypeStruct((heads, HEAD, rows), jnp.bfloat16),
            jax.ShapeDtypeStruct((heads, 1, rows), jnp.float32),
        ],
        cost_estimate=pl.CostEstimate(
            flops=16 * heads * rows * span * HEAD, bytes_accessed=16 * 2**20, transcendentals=0
        ),
    )(lengths, slopes, mixed)


def attend_back(lengths, slopes, mixed, grad, lse):
    heads, depth, rows = mixed.shape
    slots = lengths.shape[0]
    span = rows // slots
    return pl.pallas_call(
        attend_back_kernel,
        grid_spec=pltpu.PrefetchScalarGridSpec(
            num_scalar_prefetch=2,
            grid=(heads // HEADS_STEP, slots),
            in_specs=[per_head(depth, span), per_head(HEAD, span), per_head(1, span)],
            out_specs=per_head(depth, span),
        ),
        out_shape=jax.ShapeDtypeStruct(mixed.shape, jnp.bfloat16),
        cost_estimate=pl.CostEstimate(
            flops=40 * heads * rows * span * HEAD, bytes_accessed=32 * 2**20, transcendentals=0
        ),
    )(lengths, slopes, mixed, grad, lse)


def swap(value, axis):
    if axis == "y":
        return lax.ppermute(value, "col", [(i, i ^ 1) for i in range(lax.axis_size("col"))])
    step = {"core": 1, "x": 2}[axis]
    return lax.ppermute(value, "dp", [(i, i ^ step) for i in range(lax.axis_size("dp"))])


def spread(piece, order):
    held = piece[None]
    for axis in (*order, "core"):
        held = jnp.concatenate((held, swap(held, axis)), axis=0)
    return held


def collect(near, far, order):
    held = (near.astype(jnp.float32) + swap(far, "core").astype(jnp.float32)).astype(jnp.bfloat16)
    for axis in (order[1], order[0]):
        half = held.shape[0] // 2
        other = swap(held[half:], axis)
        held = (held[:half].astype(jnp.float32) + other.astype(jnp.float32)).astype(jnp.bfloat16)
    return held[0]


def places(order):
    index = jnp.arange(8)
    bit = {"core": index // 4, order[1]: index // 2 % 2, order[0]: index % 2}
    dp = lax.axis_index("dp") ^ (2 * bit["x"] + bit["core"])
    return 4 * (lax.axis_index("col") ^ bit["y"]) + dp


def stats(value):
    width = value.shape[0]
    mean = jnp.sum(value, axis=0, keepdims=True) / width
    var = jnp.sum(value * value, axis=0, keepdims=True) / width - mean * mean
    return mean, lax.rsqrt(var + EPS)


def norm_back(incoming, normed, inverse, gain):
    width = incoming.shape[0]
    scaled = incoming * gain
    first = jnp.sum(scaled, axis=0, keepdims=True) / width
    second = jnp.sum(scaled * normed, axis=0, keepdims=True) / width
    return inverse * (scaled - first - normed * second)


HEAD_ORDER = ("y", "x")
UP_ORDER = ("x", "y")


def body(
    hidden_in,
    lengths,
    ln1_gain,
    ln1_shift,
    w_qkv,
    bias_q,
    bias_v,
    w_out,
    bias_out,
    ln2_gain,
    ln2_shift,
    w_up,
    bias_up,
    w_down,
    bias_down,
    cotangent,
):
    low, f32 = jnp.bfloat16, jnp.float32
    col, dp = lax.axis_index("col"), lax.axis_index("dp")
    part, rows = hidden_in.shape[0], hidden_in.shape[1] // 2
    slots = lengths.shape[0] // 2
    lengths = lax.dynamic_slice(lengths, (col * slots,), (slots,))

    def quarter(value, axis):
        size = value.shape[axis] // 4
        return lax.dynamic_slice_in_dim(value, dp * size, size, axis)

    piece_qkv = lax.all_gather(quarter(w_qkv, 1), "row", axis=0, tiled=True)
    piece_out = lax.all_gather(quarter(w_out, 0), "row", axis=1, tiled=True)
    piece_up = lax.all_gather(quarter(w_up, 1), "row", axis=0, tiled=True)
    piece_down = lax.all_gather(quarter(w_down, 0), "row", axis=1, tiled=True)

    def both(mine, other, axis):
        return jnp.where(
            col == 0,
            jnp.concatenate((mine, other), axis=axis),
            jnp.concatenate((other, mine), axis=axis),
        )

    def to_tokens(value):
        mine = lax.dynamic_slice_in_dim(value, col * rows, rows, 1)
        send = lax.dynamic_slice_in_dim(value, (1 - col) * rows, rows, 1).astype(low)
        return both(mine, swap(send, "y").astype(f32), 0)

    def to_features(value):
        mine = lax.dynamic_slice_in_dim(value, col * part, part, 0)
        send = lax.dynamic_slice_in_dim(value, (1 - col) * part, part, 0).astype(low)
        return both(mine, swap(send, "y").astype(f32), 1)

    small_in = (
        ln1_gain, ln1_shift, bias_q, bias_v, bias_out, ln2_gain, ln2_shift, bias_down, bias_up
    )
    packed = jnp.concatenate(small_in)
    pair = both(packed[None], swap(packed, "y")[None], 0)
    cuts = [0]
    for value in small_in:
        cuts.append(cuts[-1] + value.shape[0])
    full = [pair[:, a:b].reshape(-1) for a, b in zip(cuts, cuts[1:])]
    gain1, shift1, full_q, full_v, full_out, gain2, shift2, full_down, full_up = full
    head_at, up_at = places(HEAD_ORDER), places(UP_ORDER)
    pair_heads = HEADS // 8
    bias_qv = jnp.stack(
        (full_q.reshape(HEADS, HEAD), jnp.zeros((HEADS, HEAD), f32), full_v.reshape(HEADS, HEAD)),
        axis=1,
    ).reshape(8, pair_heads * 3 * HEAD)[head_at]
    head_ids = (head_at[:, None] * pair_heads + jnp.arange(pair_heads)).reshape(HEADS)
    slopes = jnp.exp2(-8.0 * (head_ids.astype(f32) + 1.0) / HEADS)
    bias_hidden = full_up.reshape(8, -1)[up_at]

    tokens = to_tokens(hidden_in)
    wide_qkv = spread(piece_qkv, HEAD_ORDER)
    wide_out = spread(piece_out, HEAD_ORDER)
    wide_up = spread(piece_up, UP_ORDER)
    wide_down = spread(piece_down, UP_ORDER)
    grad_given = to_tokens(cotangent)

    mean1, inverse1 = stats(tokens)
    rows1 = ((tokens - mean1) * inverse1 * gain1[:, None] + shift1[:, None]).astype(low)
    mixed = (
        jnp.einsum("pkn,kt->pnt", wide_qkv, rows1, preferred_element_type=f32)
        + bias_qv[:, :, None]
    ).astype(low)
    mixed = mixed.reshape(HEADS, 3 * HEAD, rows)
    attn, lse = attend(lengths, slopes, mixed)
    attn = attn.reshape(HEADS * HEAD, rows)
    flat_out = wide_out.reshape(HEADS * HEAD, -1)
    hidden1 = (
        tokens
        + jnp.einsum("cd,ct->dt", flat_out, attn, preferred_element_type=f32)
        + full_out[:, None]
    )
    mean2, inverse2 = stats(hidden1)
    rows2 = ((hidden1 - mean2) * inverse2 * gain2[:, None] + shift2[:, None]).astype(low)
    pre = (
        jnp.einsum("pkn,kt->pnt", wide_up, rows2, preferred_element_type=f32)
        + bias_hidden[:, :, None]
    ).astype(low)
    units = pre.shape[0] * pre.shape[1]
    pre = pre.reshape(units, rows)
    gelu = partial(jax.nn.gelu, approximate=True)
    act = gelu(pre.astype(f32)).astype(low)
    flat_down = wide_down.reshape(units, -1)
    result = (
        hidden1
        + jnp.einsum("fd,ft->dt", flat_down, act, preferred_element_type=f32)
        + full_down[:, None]
    )
    hidden_out = to_features(result)

    def halves(equation, left, right, near_left, near_right):
        def one(which):
            pick = lambda value: value[which * (value.shape[0] // 2) :][: value.shape[0] // 2]
            return jnp.einsum(
                equation,
                pick(left) if near_left else left,
                pick(right) if near_right else right,
                preferred_element_type=f32,
            ).astype(low)

        far = one(1)
        return one(0), far

    grad_low = grad_given.astype(low)
    act8 = act.reshape(8, -1, rows)
    sum_down = collect(
        *halves("pft,dt->pfd", act8, grad_low, True, False), UP_ORDER
    )
    grad_act = jnp.einsum("fd,dt->ft", flat_down, grad_low, preferred_element_type=f32)
    grad_pre = jax.vjp(gelu, pre.astype(f32))[1](grad_act)[0].astype(low)
    pre8 = grad_pre.reshape(8, -1, rows)
    sum_up = collect(*halves("kt,pnt->pkn", rows2, pre8, False, True), UP_ORDER)
    grad_norm2 = jnp.einsum("pkn,pnt->kt", wide_up, pre8, preferred_element_type=f32)
    normed2 = (hidden1 - mean2) * inverse2
    grad_hidden1 = grad_given + norm_back(grad_norm2, normed2, inverse2, gain2[:, None])
    branch_low = grad_hidden1.astype(low)
    grad_attn = jnp.einsum("cd,dt->ct", flat_out, branch_low, preferred_element_type=f32)
    grad_attn = grad_attn.astype(low).reshape(HEADS, HEAD, rows)
    sum_out = collect(
        *halves("pct,dt->pcd", attn.reshape(8, -1, rows), branch_low, True, False), HEAD_ORDER
    )
    grad_mixed = attend_back(lengths, slopes, mixed, grad_attn, lse)
    mixed8 = grad_mixed.reshape(8, -1, rows)
    sum_qkv = collect(*halves("kt,pnt->pkn", rows1, mixed8, False, True), HEAD_ORDER)
    grad_norm1 = jnp.einsum("pkn,pnt->kt", wide_qkv, mixed8, preferred_element_type=f32)
    normed1 = (tokens - mean1) * inverse1
    grad_input = to_features(
        grad_hidden1 + norm_back(grad_norm1, normed1, inverse1, gain1[:, None])
    )

    def total(value):
        return jnp.sum(value, axis=1, dtype=f32)

    head_back, up_back = jnp.argsort(head_at), jnp.argsort(up_at)
    mixed_sums = jnp.sum(grad_mixed, axis=2, dtype=f32).reshape(8, pair_heads, 3, HEAD)[head_back]
    early = (
        total(grad_hidden1),
        total(grad_norm2 * normed2),
        total(grad_norm2),
        total(grad_pre).reshape(8, -1)[up_back].reshape(-1),
        total(grad_given),
    )
    late = (
        total(grad_norm1 * normed1),
        total(grad_norm1),
        mixed_sums[:, :, 0].reshape(-1),
        mixed_sums[:, :, 2].reshape(-1),
    )

    def reduce_small(values):
        summed = lax.psum(jnp.concatenate([v.reshape(2, -1) for v in values], axis=1),
                          ("dp", "row", "col"))
        mine = lax.dynamic_slice_in_dim(summed, col, 1, 0)[0]
        parts, at = [], 0
        for value in values:
            parts.append(mine[at : at + value.shape[0] // 2])
            at += value.shape[0] // 2
        return parts

    g_bias_out, g_gain2, g_shift2, g_bias_up, g_bias_down = reduce_small(early)
    g_gain1, g_shift1, g_bias_q, g_bias_v = reduce_small(late)

    def finish(value, row_axis):
        mine = lax.psum_scatter(value, "row", scatter_dimension=row_axis, tiled=True)
        return lax.all_gather(mine, "dp", axis=1 - row_axis, tiled=True).astype(f32)

    return (
        hidden_out,
        grad_input,
        g_gain1,
        g_shift1,
        finish(sum_qkv, 0),
        g_bias_q,
        g_bias_v,
        finish(sum_out, 1),
        g_bias_out,
        g_gain2,
        g_shift2,
        finish(sum_up, 0),
        g_bias_up,
        finish(sum_down, 1),
        g_bias_down,
    )


def solution(mesh):
    pairs = mesh.shape["col"] == 2 and mesh.shape["dp"] == 4
    return jax.shard_map(
        body if pairs else wide_body,
        mesh=mesh,
        in_specs=(
            P("col", ("dp", "row")),
            P(("dp", "row")),
            P("col"),
            P("col"),
            P("row", "col"),
            P("col"),
            P("col"),
            P("col", "row"),
            P("col"),
            P("col"),
            P("col"),
            P("row", "col"),
            P("col"),
            P("col", "row"),
            P("col"),
            P("col", ("dp", "row")),
        ),
        out_specs=(
            P("col", ("dp", "row")),
            P("col", ("dp", "row")),
            P("col"),
            P("col"),
            P("row", "col"),
            P("col"),
            P("col"),
            P("col", "row"),
            P("col"),
            P("col"),
            P("col"),
            P("row", "col"),
            P("col"),
            P("col", "row"),
            P("col"),
        ),
        check_vma=False,
    )
```
